128 devices in a mesh: branch: 4 (over z), ctx: 32 (over y, x, core).
Axes of the slice: x: 4, y: 4, z: 4, core: 2. Of those that a mesh axis runs over, the one named last changes fastest.
Arguments:
- summary_q: bfloat16 [65536, 2560], P(('branch', 'ctx')), may hold values from -32 to 32
- summary_kv: bfloat16 [65536, 2, 512], P(('branch', 'ctx')), may hold values from -12 to 12
- kv_cache: bfloat16 [512, 2, 128, 512], P(('branch', 'ctx')), may hold values from -9 to 9
- block_slot: int32 [512], replicated, may hold values from 0 to 511, as said below
- tile_blocks: int32 [512, 8], P(('branch', 'ctx')), may hold values from 0 to 511, as said below
- tile_count: int32 [512], P(('branch', 'ctx')), may hold values from 2 to 8
Outputs:
- attended: bfloat16 [65536, 2560], P(('branch', 'ctx'))
The draws below stay inside these ranges and needn't reach their ends.
Inputs may be any that keep to these rules, and one draw needn't show every extreme that they name: `block_slot`: each slot number appears once; slot s lies on the device of index s // 4 along branch+ctx. `tile_blocks`: among the first tile_count[t] entries of the 4 tiles of one device, at most 2 are stored on devices of one ctx index and at most 1 on one device; entries after tile_count[t] are not read.
All inputs are finite; a program needn't handle non-finite values.
Results may differ from the reference program's by a relative error of at most 0.0045.
Values may be sent and summed in bfloat16 or wider, within the bound.
No kernel may reach another device: no remote copies, remote signals or barrier semaphores. Data moves between devices by JAX's collectives and lax.ppermute only.
A program may use at most 192 MiB of HBM per device.

```python
import jax
import jax.numpy as jnp
from jax import lax

HEAD = 128
KVH = 4
REP = 5
BLOCK = 128
TILE = 128
TILES_DEV = 4
REQ_TILES = 32
BLK_DEV = 4
GROUPS = 4
SHARDS = 32
DEVS = 128
QW = 2560
KVW = 512
LIST = 8
CAPB = 2
TILES = 512
TOKENS = 65536
BLOCKS = 512


def plan_lists(key):
    base_key = jax.random.fold_in(key, 1013)
    subkeys = jax.random.split(base_key, 11)
    block_slot = jax.random.permutation(subkeys[0], BLOCKS).astype(jnp.int32)
    block_of_slot = jnp.argsort(block_slot).astype(jnp.int32)
    per_dev = TILES_DEV * LIST
    hot_col = jax.random.randint(subkeys[1], (), 0, SHARDS)
    hot_row = jax.random.randint(subkeys[2], (), 0, GROUPS)
    hot_tile = jax.random.randint(subkeys[3], (DEVS, 1), 0, TILES_DEV)
    positions = jnp.arange(per_dev, dtype=jnp.int32)[None, :]
    tile_of = positions // LIST
    within = positions % LIST
    is_hot = (tile_of == hot_tile) & (within < CAPB)
    rest_rank = jnp.cumsum(jnp.where(is_hot, 0, 1), axis=1) - 1
    rest_rank = jnp.maximum(rest_rank, 0)
    group_count = (per_dev - CAPB + CAPB - 1) // CAPB
    offset = jax.random.randint(subkeys[4], (DEVS, 1), 0, SHARDS - group_count)
    group_of = rest_rank // CAPB
    member = rest_rank % CAPB
    column = jnp.where(is_hot, hot_col, (hot_col + 1 + offset + group_of) % SHARDS)
    row_start = jax.random.randint(subkeys[5], (DEVS, per_dev), 0, GROUPS)
    start_row = jnp.take_along_axis(row_start, group_of, axis=1)
    row_of = jnp.where(is_hot, (hot_row + within) % GROUPS, (start_row + member) % GROUPS)
    local_slot = jax.random.randint(subkeys[6], (DEVS, per_dev), 0, BLK_DEV)
    stored = (row_of * SHARDS + column) * BLK_DEV + local_slot
    tile_blocks = block_of_slot[stored].reshape(TILES, LIST).astype(jnp.int32)
    heavy_dev = jax.random.randint(subkeys[7], (DEVS, 1), 0, 4) == 0
    light_count = jax.random.randint(subkeys[8], (DEVS, TILES_DEV), max(CAPB, LIST // 2), LIST + 1)
    counts = jnp.where(heavy_dev, LIST, light_count).reshape(TILES)
    full_tile = jax.random.randint(subkeys[9], (), 0, TILES)
    low_tile = (full_tile + 1 + jax.random.randint(subkeys[10], (), 0, TILES - 1)) % TILES
    counts = counts.at[full_tile].set(LIST).at[low_tile].set(CAPB)
    return (block_slot, tile_blocks, counts.astype(jnp.int32))


def draw_summary_q(key, part):
    bulk_key = jax.random.fold_in(key, 31)
    drawn = jax.random.truncated_normal(bulk_key, -6.0, 6.0, (TOKENS, QW), jnp.float32)
    return drawn.astype(jnp.bfloat16)


def draw_summary_kv(key, part):
    bulk_key = jax.random.fold_in(key, 47)
    drawn = 2.0 * jax.random.truncated_normal(bulk_key, -6.0, 6.0, (TOKENS, 2, KVW), jnp.float32)
    return drawn.astype(jnp.bfloat16)


def draw_block_slot(key, part):
    return plan_lists(key)[0]


def draw_tile_blocks(key, part):
    return plan_lists(key)[1]


def draw_tile_count(key, part):
    return plan_lists(key)[2]


def block_levels(rng, shape, shards, smallest, largest):
    factor_of, own = 1.0, jax.random.fold_in(rng, 6)
    for dim, parts in shards:
        steps = jnp.exp(jax.random.uniform(jax.random.fold_in(own, dim), (parts,), jnp.float32, smallest / len(shards), largest / len(shards)))
        factor_of = factor_of * jnp.repeat(steps, shape[dim] // parts).reshape([-1 if axis == dim else 1 for axis in range(len(shape))])
    return factor_of


def normal_values(key, shape, width, most, pieces=(), held_as=jnp.bfloat16):
    values = jax.random.normal(key, shape, jnp.float32) * width
    if len(pieces) > 0:
        values = block_levels(key, shape, pieces, -0.22, 0.18) * values
    return jnp.clip(values, min=-most, max=most).astype(held_as)


def setup_inputs(seed: int = 0) -> dict:
    seeds = jax.random.split(jax.random.key(seed), 7)
    return {
        "summary_q": draw_summary_q(jax.random.fold_in(seeds[6], 71), 0),
        "summary_kv": draw_summary_kv(jax.random.fold_in(seeds[6], 71), 0),
        "kv_cache": normal_values(seeds[2], (BLOCKS, 2, BLOCK, KVW), 1.5, 9.0, ((0, 128),)),
        "block_slot": draw_block_slot(jax.random.fold_in(seeds[6], 71), 0),
        "tile_blocks": draw_tile_blocks(jax.random.fold_in(seeds[6], 71), 0),
        "tile_count": draw_tile_count(jax.random.fold_in(seeds[6], 71), 0),
    }


def reference(summary_q, summary_kv, kv_cache, block_slot, tile_blocks, tile_count):
    tile_num = tile_blocks.shape[0]
    list_len = tile_blocks.shape[1]
    span_len = REQ_TILES * TILE
    queries = summary_q.reshape(tile_num, TILE, KVH, REP, HEAD)
    rolled_kv = jnp.roll(summary_kv, -TILES_DEV * TILE, axis=0)
    request_kv = rolled_kv.reshape(tile_num // REQ_TILES, span_len, 2, KVH, HEAD)
    tile_ids = jnp.arange(tile_num, dtype=jnp.int32)
    key_pos = jnp.arange(span_len, dtype=jnp.int32)
    score_scale = HEAD ** -0.5

    def one_tile(packed):
        query_tile, listed, count_live, tile_id = packed
        moved_id = (tile_id - TILES_DEV + tile_num) % tile_num
        span_kv = request_kv[moved_id // REQ_TILES]
        query_pos = (moved_id % REQ_TILES) * TILE + jnp.arange(TILE, dtype=jnp.int32)
        summary_mask = key_pos[None, :] <= query_pos[:, None]
        stored_at = block_slot[listed]
        fetched = kv_cache[stored_at]
        branch_keys = fetched[:, 0].reshape(list_len * BLOCK, KVH, HEAD)
        branch_values = fetched[:, 1].reshape(list_len * BLOCK, KVH, HEAD)
        key_rows = jnp.concatenate([span_kv[:, 0], branch_keys], axis=0).astype(jnp.float32)
        value_rows = jnp.concatenate([span_kv[:, 1], branch_values], axis=0).astype(jnp.float32)
        live_block = jnp.arange(list_len, dtype=jnp.int32) < count_live
        live_keys = jnp.repeat(live_block, BLOCK)
        key_mask = jnp.concatenate([summary_mask, jnp.broadcast_to(live_keys[None, :], (TILE, list_len * BLOCK))], axis=1)
        scores = jnp.einsum("qgrd,kgd->grqk", query_tile.astype(jnp.float32), key_rows) * score_scale
        scores = jnp.where(key_mask[None, None], scores, -jnp.inf)
        row_max = jnp.max(scores, axis=-1, keepdims=True)
        weights = jnp.exp(scores - row_max)
        row_sum = jnp.sum(weights, axis=-1)
        rounded = lax.optimization_barrier(weights.astype(jnp.bfloat16)).astype(jnp.float32)
        attended = jnp.einsum("grqk,kgd->qgrd", rounded, value_rows) / jnp.transpose(row_sum, (2, 0, 1))[..., None]
        return attended.reshape(TILE, KVH * REP * HEAD).astype(jnp.bfloat16)

    result = lax.map(one_tile, (queries, tile_blocks, tile_count, tile_ids))
    return result.reshape(tile_num * TILE, KVH * REP * HEAD)
```

```python
import functools
import math

import jax
import jax.numpy as jnp
from jax import lax
from jax.experimental import pallas as pl
from jax.experimental.pallas import tpu as pltpu
from jax.sharding import PartitionSpec as P

HEAD = 128
REQ_TILES = 32
EXP_SCALE = math.log2(math.e) / math.sqrt(HEAD)
CAP = 2


def request_table(dest_index, live_mask, count_dest, capacity, payload):
    onehot = (
        (dest_index[:, None] == jnp.arange(count_dest, dtype=jnp.int32)[None, :])
        & live_mask[:, None]
    ).astype(jnp.int32)
    rank_within = jnp.sum(onehot * (jnp.cumsum(onehot, axis=0) - 1), axis=1)
    position = dest_index * capacity + rank_within
    target = jnp.where(live_mask, position, -1)
    slot_ids = jnp.arange(count_dest * capacity, dtype=jnp.int32)
    requests = jnp.max(
        jnp.where(target[:, None] == slot_ids[None, :], payload[:, None], -1), axis=0
    )
    return (requests.reshape(count_dest, capacity), position)


def weigh(queries, keys, values_one, old_max, old_acc, mask):
    scores = lax.dot_general(
        queries, keys, (((1,), (1,)), ((), ())), preferred_element_type=jnp.float32
    )
    if mask is not None:
        scores = jnp.where(mask, scores, -jnp.inf)
    top = jnp.max(scores, axis=1, keepdims=True)
    new_max = top if old_max is None else jnp.maximum(old_max, top)
    weights = jnp.exp2((scores - new_max) * EXP_SCALE).astype(jnp.bfloat16)
    acc = jnp.dot(weights, values_one, preferred_element_type=jnp.float32)
    if old_max is not None:
        acc = acc + old_acc * jnp.exp2((old_max - new_max) * EXP_SCALE)
    return new_max, acc


def stack_heads(q_tile, repeat):
    return jnp.concatenate([q_tile[:, r * HEAD : (r + 1) * HEAD] for r in range(repeat)], axis=0)


def span_kernel(repeat, tile_rows, place_ref, q_ref, own_ref, *rest):
    earlier, (state_ref, key_buf, value_buf) = rest[:-3], rest[-3:]
    tiles = q_ref.shape[0] // tile_rows
    ones = jnp.ones((own_ref.shape[1], HEAD), jnp.bfloat16)
    for slot, ref in enumerate((own_ref, *earlier)):
        key_buf[slot] = ref[0]
        value_buf[slot, :, :HEAD] = ref[1]
        value_buf[slot, :, HEAD:] = ones
    wide = repeat * tile_rows
    for t in range(tiles):
        queries = stack_heads(q_ref[t * tile_rows : (t + 1) * tile_rows, :], repeat)
        seen = (t + 1) * tile_rows
        row = lax.rem(lax.broadcasted_iota(jnp.int32, (wide, seen), 0), tile_rows) + t * tile_rows
        col = lax.broadcasted_iota(jnp.int32, (wide, seen), 1)
        top, acc = weigh(
            queries, key_buf[0, :seen], value_buf[0, :seen], None, None, col <= row
        )
        state_ref[0, t, :, : 2 * HEAD] = acc
        state_ref[0, t, :, 2 * HEAD :] = jnp.broadcast_to(top, (wide, HEAD))

    def take(step, carry):
        slot, t = step // tiles + 1, lax.rem(step, tiles)
        rows = pl.ds(pl.multiple_of(t * tile_rows, tile_rows), tile_rows)
        queries = stack_heads(q_ref[rows, :], repeat)
        top, acc = weigh(
            queries,
            key_buf[slot],
            value_buf[slot],
            state_ref[0, t, :, 2 * HEAD : 2 * HEAD + 1],
            state_ref[0, t, :, : 2 * HEAD],
            None,
        )
        state_ref[0, t, :, : 2 * HEAD] = acc
        state_ref[0, t, :, 2 * HEAD :] = jnp.broadcast_to(top, (wide, HEAD))
        return carry

    lax.fori_loop(0, place_ref[0] * tiles, take, 0)


def span_attention(place, queries, own, earlier, tile_num):
    rows, width = queries.shape
    kv_heads = own.shape[2] // HEAD
    group = width // kv_heads
    repeat = group // HEAD
    tile_rows = rows // tile_num
    wide = repeat * tile_rows
    kv_spec = pl.BlockSpec((2, rows, HEAD), lambda g, place: (0, 0, g))
    slots = 1 + len(earlier)
    return pl.pallas_call(
        functools.partial(span_kernel, repeat, tile_rows),
        out_shape=jax.ShapeDtypeStruct((kv_heads, tile_num, wide, 3 * HEAD), jnp.float32),
        grid_spec=pltpu.PrefetchScalarGridSpec(
            num_scalar_prefetch=1,
            grid=(kv_heads,),
            in_specs=[pl.BlockSpec((rows, group), lambda g, place: (0, g))] + [kv_spec] * slots,
            out_specs=pl.BlockSpec((1, tile_num, wide, 3 * HEAD), lambda g, place: (g, 0, 0, 0)),
            scratch_shapes=[
                pltpu.VMEM((slots, rows, HEAD), jnp.bfloat16),
                pltpu.VMEM((slots, rows, 2 * HEAD), jnp.bfloat16),
            ],
        ),
        compiler_params=pltpu.CompilerParams(vmem_limit_bytes=56 * 2**20),
        cost_estimate=pl.CostEstimate(
            flops=4 * rows * width * rows * (slots // 2 + 1),
            bytes_accessed=rows * width * 2 + slots * rows * 4 * kv_heads * HEAD + rows * width * 12,
            transcendentals=rows * width // HEAD * rows * (slots // 2 + 1),
        ),
    )(place, queries, own, *earlier)


def listed_kernel(repeat, tile_rows, per_step, count_ref, pos_ref, q_ref, state_ref, block_ref, *rest):
    out_ref = rest[-1]
    t = pl.program_id(0)
    wide = repeat * tile_rows
    block_len = block_ref.shape[2]
    queries = stack_heads(q_ref[...], repeat)
    ones = jnp.ones((per_step * block_len, HEAD), jnp.bfloat16)
    count = count_ref[t]

    def take(step, carry):
        top, acc = carry
        first = step * per_step
        slots = [pos_ref[t, first + i] for i in range(per_step)]
        keys = jnp.concatenate([block_ref[s, 0] for s in slots], axis=0)
        values = jnp.concatenate([block_ref[s, 1] for s in slots], axis=0)
        col = lax.broadcasted_iota(jnp.int32, (1, per_step * block_len), 1)
        mask = col < (count - first) * block_len
        return weigh(
            queries, keys, jnp.concatenate([values, ones], axis=1), top, acc, mask
        )

    top, acc = state_ref[0, 0, :, 2 * HEAD : 2 * HEAD + 1], state_ref[0, 0, :, : 2 * HEAD]
    steps = (count + per_step - 1) // per_step
    top, acc = lax.fori_loop(0, steps, take, (top, acc))
    result = (acc[:, :HEAD] / acc[:, HEAD:]).astype(jnp.bfloat16)
    for r in range(repeat):
        out_ref[:, r * HEAD : (r + 1) * HEAD] = result[r * tile_rows : (r + 1) * tile_rows, :]


def listed_attention(head, counts, position, queries, state, blocks, partial_out):
    rows, width = queries.shape
    kv_heads, tile_num, wide, _ = state.shape
    group = width // kv_heads
    repeat = group // HEAD
    tile_rows = rows // tile_num
    in_specs = [
        pl.BlockSpec((tile_rows, group), lambda t, c, p: (t, head)),
        pl.BlockSpec((1, 1, wide, 3 * HEAD), lambda t, c, p: (head, t, 0, 0)),
        pl.BlockSpec(blocks.shape, lambda t, c, p: (0, 0, 0, 0)),
    ]
    operands = [counts, position, queries, state, blocks]
    aliases = {}
    if partial_out is not None:
        in_specs.append(pl.BlockSpec(memory_space=pl.ANY))
        operands.append(partial_out)
        aliases = {5: 0}
    keys = position.shape[1] * blocks.shape[2]
    return pl.pallas_call(
        functools.partial(listed_kernel, repeat, tile_rows, 4),
        out_shape=jax.ShapeDtypeStruct((rows, width), jnp.bfloat16),
        grid_spec=pltpu.PrefetchScalarGridSpec(
            num_scalar_prefetch=2,
            grid=(tile_num,),
            in_specs=in_specs,
            out_specs=pl.BlockSpec((tile_rows, group), lambda t, c, p: (t, head)),
        ),
        input_output_aliases=aliases,
        compiler_params=pltpu.CompilerParams(vmem_limit_bytes=40 * 2**20),
        cost_estimate=pl.CostEstimate(
            flops=4 * rows * group * keys,
            bytes_accessed=rows * group * 16 + blocks.size * 2,
            transcendentals=rows * repeat * keys,
        ),
    )(*operands)


def local(summary_q, summary_kv, kv_cache, block_slot, tile_blocks, tile_count):
    shards = lax.axis_size("ctx")
    groups = lax.axis_size("branch")
    devices = shards * groups
    tile_num, list_len = tile_blocks.shape
    blk_dev = kv_cache.shape[0]
    kv_heads = kv_cache.shape[3] // HEAD
    req_devs = REQ_TILES // tile_num
    entries = tile_blocks.reshape(-1)
    live_mask = (jnp.arange(list_len, dtype=jnp.int32)[None, :] < tile_count[:, None]).reshape(-1)
    block_ids = jnp.arange(block_slot.shape[0], dtype=jnp.int32)
    stored_at = jnp.sum(
        jnp.where(entries[:, None] == block_ids[None, :], block_slot[None, :], 0), axis=1
    )
    owner_dev = stored_at // blk_dev
    requests, position = request_table(
        owner_dev % shards,
        live_mask,
        shards,
        CAP,
        owner_dev // shards * blk_dev + stored_at % blk_dev,
    )
    asked = lax.all_to_all(requests, "ctx", split_axis=0, concat_axis=0, tiled=True)
    asked = jnp.maximum(asked, 0).reshape(-1)
    position = jnp.where(live_mask, position, 0).reshape(tile_num, list_len)
    flat_index = lax.axis_index("branch") * shards + lax.axis_index("ctx")
    place = (flat_index - 1 + req_devs) % req_devs
    own = summary_kv.transpose(1, 0, 2)
    earlier = []
    for distance in range(1, req_devs):
        pairs = [
            (source, (source + distance) % devices)
            for source in range(devices)
            if (source + distance - 1) % req_devs >= distance
        ]
        earlier.append(lax.ppermute(own, ("branch", "ctx"), pairs))
    state = span_attention(place[None], summary_q, own, earlier, tile_num)
    out = None
    for head in range(kv_heads):
        part = kv_cache[..., head * HEAD : (head + 1) * HEAD]
        column = lax.all_gather(part, "branch", axis=0, tiled=True)
        payload = column[asked]
        received = lax.all_to_all(payload, "ctx", split_axis=0, concat_axis=0, tiled=True)
        out = listed_attention(head, tile_count, position, summary_q, state, received, out)
    return out


def solution(mesh):
    in_specs = (
        P(("branch", "ctx"), None),
        P(("branch", "ctx"), None, None),
        P(("branch", "ctx"), None, None, None),
        P(),
        P(("branch", "ctx"), None),
        P(("branch", "ctx")),
    )
    out_specs = P(("branch", "ctx"), None)
    return jax.shard_map(local, mesh=mesh, in_specs=in_specs, out_specs=out_specs, check_vma=False)
```

```python
import functools
import math

import jax
import jax.numpy as jnp
from jax import lax
from jax.experimental import pallas as pl
from jax.experimental.pallas import tpu as pltpu
from jax.sharding import Mesh
from jax.sharding import PartitionSpec as P


HEAD = 128
REQ_TILES = 32
EXP_SCALE = math.log2(math.e) / math.sqrt(HEAD)
ALL = ("z", "y", "x", "c")
PLANE = ("y", "x", "c")
CAP = 2
CHUNKS = ((0,), (1, 2), (3,))
PLAN = ((), ((0, 1), (2, 3), 0), (1, 2, 3))


def request_table(dest_index, live_mask, count_dest, capacity, payload):
    onehot = (
        (dest_index[:, None] == jnp.arange(count_dest, dtype=jnp.int32)[None, :])
        & live_mask[:, None]
    ).astype(jnp.int32)
    rank_within = jnp.sum(onehot * (jnp.cumsum(onehot, axis=0) - 1), axis=1)
    target = jnp.where(live_mask, dest_index * capacity + rank_within, -1)
    slot_ids = jnp.arange(count_dest * capacity, dtype=jnp.int32)
    requests = jnp.max(
        jnp.where(target[:, None] == slot_ids[None, :], payload[:, None], 0), axis=0
    )
    return (requests.reshape(count_dest, capacity), dest_index * capacity + rank_within)


def score(queries, keys):
    return lax.dot_general(
        queries, keys, (((1,), (1,)), ((), ())), preferred_element_type=jnp.float32
    )


def weigh(scores, values_one, old_max, old_acc, masks):
    pieces = [scores[:, i : i + HEAD] for i in range(0, scores.shape[1], HEAD)]
    pieces = [
        piece if mask is None else jnp.where(mask, piece, -jnp.inf)
        for piece, mask in zip(pieces, masks, strict=True)
    ]
    top = jnp.max(functools.reduce(jnp.maximum, pieces), axis=1, keepdims=True)
    top = jnp.broadcast_to(top, pieces[0].shape)
    new_max = top if old_max is None else jnp.maximum(old_max, top)
    weights = [
        jnp.exp2((piece - new_max) * EXP_SCALE).astype(jnp.bfloat16) for piece in pieces
    ]
    acc = jnp.dot(
        jnp.concatenate(weights, axis=1), values_one, preferred_element_type=jnp.float32
    )
    if old_max is None:
        return new_max, acc[:, :HEAD], acc[:, HEAD:]
    fade = jnp.exp2((old_max - new_max) * EXP_SCALE)
    total, row_sum = old_acc
    return new_max, acc[:, :HEAD] + total * fade, acc[:, HEAD:] + row_sum * fade


def stack_heads(q_tile, repeat):
    return jnp.concatenate([q_tile[:, r * HEAD : (r + 1) * HEAD] for r in range(repeat)], axis=0)


def span_kernel(repeat, tile_rows, place_ref, q_ref, own_ref, *rest):
    earlier, (state_ref, key_buf, value_buf) = rest[:-3], rest[-3:]
    tiles = q_ref.shape[0] // tile_rows
    ones = jnp.ones((own_ref.shape[1], HEAD), jnp.bfloat16)
    other_ref, same_refs, first_ref = earlier[0], earlier[1:-1], earlier[-1]
    spans = [own_ref]
    for i, same_ref in enumerate(same_refs):
        spans += [other_ref.at[i], same_ref]
    for slot, ref in enumerate((*spans, first_ref)):
        key_buf[slot] = ref[0]
        value_buf[slot, :, :HEAD] = ref[1]
        value_buf[slot, :, HEAD:] = ones
    wide = repeat * tile_rows

    def own_scores(t):
        queries = stack_heads(q_ref[t * tile_rows : (t + 1) * tile_rows, :], repeat)
        return score(queries, key_buf[0, : (t + 1) * tile_rows])

    def put(t, state):
        for i, part in enumerate((*state[1:], state[0])):
            state_ref[0, t, :, i * HEAD : (i + 1) * HEAD] = part

    row = lax.rem(lax.broadcasted_iota(jnp.int32, (wide, tile_rows), 0), tile_rows)
    diagonal = lax.broadcasted_iota(jnp.int32, (wide, tile_rows), 1) <= row
    ahead = own_scores(0)
    for t in range(tiles):
        scores = ahead
        if t + 1 < tiles:
            ahead = own_scores(t + 1)
        masks = [None] * t + [diagonal]
        put(t, weigh(scores, value_buf[0, : (t + 1) * tile_rows], None, None, masks))

    def take(slot, carry):
        keys, values_one = key_buf[slot], value_buf[slot]

        def slot_scores(t):
            queries = stack_heads(q_ref[t * tile_rows : (t + 1) * tile_rows, :], repeat)
            return score(queries, keys)

        ahead = slot_scores(0)
        for t in range(tiles):
            scores = ahead
            if t + 1 < tiles:
                ahead = slot_scores(t + 1)
            old = [state_ref[0, t, :, i * HEAD : (i + 1) * HEAD] for i in range(3)]
            put(t, weigh(scores, values_one, old[2], old[:2], [None] * tiles))
        return carry

    lax.fori_loop(1, place_ref[0] + 1, take, 0)


def span_attention(heads, place, queries, own, earlier, tile_num):
    rows, width = queries.shape
    kv_heads = own.shape[2] // HEAD
    group = width // kv_heads
    repeat = group // HEAD
    tile_rows = rows // tile_num
    wide = repeat * tile_rows
    kv_spec = pl.BlockSpec((2, rows, HEAD), lambda g, place: (0, 0, heads[0] + g))
    other_spec = pl.BlockSpec(
        (earlier[0].shape[0], 2, rows, HEAD), lambda g, place: (0, 0, 0, heads[0] + g)
    )
    slots = len(earlier) + earlier[0].shape[0]
    return pl.pallas_call(
        functools.partial(span_kernel, repeat, tile_rows),
        out_shape=jax.ShapeDtypeStruct((len(heads), tile_num, wide, 3 * HEAD), jnp.float32),
        grid_spec=pltpu.PrefetchScalarGridSpec(
            num_scalar_prefetch=1,
            grid=(len(heads),),
            in_specs=[pl.BlockSpec((rows, group), lambda g, place: (0, heads[0] + g))]
            + [kv_spec, other_spec] + [kv_spec] * (len(earlier) - 1),
            out_specs=pl.BlockSpec((1, tile_num, wide, 3 * HEAD), lambda g, place: (g, 0, 0, 0)),
            scratch_shapes=[
                pltpu.VMEM((slots, rows, HEAD), jnp.bfloat16),
                pltpu.VMEM((slots, rows, 2 * HEAD), jnp.bfloat16),
            ],
        ),
        compiler_params=pltpu.CompilerParams(vmem_limit_bytes=56 * 2**20),
        cost_estimate=pl.CostEstimate(
            flops=4 * len(heads) * rows * group * rows * slots,
            bytes_accessed=len(heads) * (rows * group * 14 + slots * rows * 4 * HEAD),
            transcendentals=len(heads) * rows * repeat * rows * slots,
        ),
    )(place, queries, own, *earlier)


def listed_kernel(repeat, tile_rows, count_ref, pos_ref, q_ref, state_ref, block_ref, *rest):
    out_ref = rest[-1]
    tiles = q_ref.shape[0] // tile_rows
    list_len = pos_ref.shape[1]
    block_len = block_ref.shape[2]
    ones = jnp.ones((list_len * block_len, HEAD), jnp.bfloat16)

    def listed(t, kind):
        return jnp.concatenate([block_ref[pos_ref[t, i], kind] for i in range(list_len)], axis=0)

    def tile_scores(t):
        queries = stack_heads(q_ref[t * tile_rows : (t + 1) * tile_rows, :], repeat)
        return score(queries, listed(t, 0))

    ahead = tile_scores(0)
    for t in range(tiles):
        scores = ahead
        if t + 1 < tiles:
            ahead = tile_scores(t + 1)
        masks = [i < count_ref[t] for i in range(list_len)]
        old = [state_ref[0, t, :, i * HEAD : (i + 1) * HEAD] for i in range(3)]
        values_one = jnp.concatenate([listed(t, 1), ones], axis=1)
        _, total, row_sum = weigh(scores, values_one, old[2], old[:2], masks)
        result = (total / row_sum).astype(jnp.bfloat16)
        for r in range(repeat):
            out_ref[t * tile_rows : (t + 1) * tile_rows, r * HEAD : (r + 1) * HEAD] = result[
                r * tile_rows : (r + 1) * tile_rows, :
            ]


def listed_attention(head, state_row, counts, position, queries, state, blocks, lane, partial_out):
    rows, width = queries.shape
    _, tile_num, wide, _ = state.shape
    group = wide * tile_num // rows * HEAD
    repeat = group // HEAD
    tile_rows = rows // tile_num
    in_specs = [
        pl.BlockSpec((rows, group), lambda t, c, p: (0, head)),
        pl.BlockSpec((1, tile_num, wide, 3 * HEAD), lambda t, c, p: (state_row, 0, 0, 0)),
        pl.BlockSpec((*blocks.shape[:3], HEAD), lambda t, c, p: (0, 0, 0, lane)),
    ]
    operands = [counts, position, queries, state, blocks]
    aliases = {}
    if partial_out is not None:
        in_specs.append(pl.BlockSpec(memory_space=pl.ANY))
        operands.append(partial_out)
        aliases = {5: 0}
    keys = position.shape[1] * blocks.shape[2]
    return pl.pallas_call(
        functools.partial(listed_kernel, repeat, tile_rows),
        out_shape=jax.ShapeDtypeStruct((rows, width), jnp.bfloat16),
        grid_spec=pltpu.PrefetchScalarGridSpec(
            num_scalar_prefetch=2,
            grid=(1,),
            in_specs=in_specs,
            out_specs=pl.BlockSpec((rows, group), lambda t, c, p: (0, head)),
        ),
        input_output_aliases=aliases,
        compiler_params=pltpu.CompilerParams(vmem_limit_bytes=40 * 2**20),
        cost_estimate=pl.CostEstimate(
            flops=4 * rows * group * keys,
            bytes_accessed=rows * group * 16 + blocks.size * 2,
            transcendentals=rows * repeat * keys,
        ),
    )(*operands)


def local(summary_q, summary_kv, kv_cache, block_slot, tile_blocks, tile_count):
    plane, devices = lax.axis_size(PLANE), lax.axis_size(ALL)
    tile_num, list_len = tile_blocks.shape
    blk_dev = kv_cache.shape[0]
    req_devs = REQ_TILES // tile_num
    flat_index = lax.axis_index(ALL)
    entries = tile_blocks.reshape(-1)
    live_mask = (jnp.arange(list_len, dtype=jnp.int32)[None, :] < tile_count[:, None]).reshape(-1)
    block_ids = jnp.arange(block_slot.shape[0], dtype=jnp.int32)
    stored_at = jnp.sum(
        jnp.where(entries[:, None] == block_ids[None, :], block_slot[None, :], 0), axis=1
    )
    owner_dev = stored_at // blk_dev
    requests, position = request_table(
        owner_dev % plane,
        live_mask,
        plane,
        CAP,
        owner_dev // plane * blk_dev + stored_at % blk_dev,
    )
    asked = lax.all_to_all(requests, PLANE, split_axis=0, concat_axis=0, tiled=True)
    position = jnp.where(live_mask, position, 0).reshape(tile_num, list_len)
    place = (flat_index - 1 + req_devs) % req_devs
    own, asked = lax.optimization_barrier((summary_kv.transpose(1, 0, 2), asked))
    asked = asked.reshape(-1)

    def ahead(value, distance, takes):
        pairs = [
            (source, (source + distance) % devices)
            for source in range(devices)
            if takes((source - 1) % req_devs)
        ]
        return lax.ppermute(value, ALL, pairs)

    core = lax.axis_index("c")
    second = ahead(own, 2, lambda p: p + 2 <= req_devs)
    sixth = ahead(own, 6, lambda p: p + 6 <= req_devs)
    first = ahead(own, req_devs - 1, lambda p: p == 0)
    fourth = ahead(second, 2, lambda p: 2 <= p <= req_devs - 2)
    same = [second, fourth, sixth]
    give = [jnp.where(core == 0, a, b) for a, b in zip([own, *same[:-1]], same, strict=True)]
    other = lax.ppermute(jnp.stack(give), "c", [(0, 1), (1, 0)])
    earlier = [other, *same, first]
    columns = [
        lax.all_gather(
            kv_cache[..., heads[0] * HEAD : (heads[-1] + 1) * HEAD], "z", axis=0, tiled=True
        )
        for heads in CHUNKS
    ]
    states, received, out = [], {}, None
    for turn, heads in enumerate(CHUNKS):
        column = columns[turn]
        if turn > 0:
            column, states, out = lax.optimization_barrier((column, states, out))
        arrived = lax.all_to_all(column[asked], PLANE, split_axis=0, concat_axis=0, tiled=True)
        for i, head in enumerate(heads):
            received[head] = (arrived, i)
        for task in PLAN[turn]:
            if isinstance(task, tuple):
                state = span_attention(task, place[None], summary_q, own, earlier, tile_num)
                states = states + [state]
            else:
                out = listed_attention(
                    task,
                    task % 2,
                    tile_count,
                    position,
                    summary_q,
                    states[task // 2],
                    *received[task],
                    out,
                )
    return out


def solution(mesh):
    grid = Mesh(mesh.devices.reshape(4, 4, 4, 2), ALL)
    in_specs = (P(ALL, None), P(ALL, None, None), P(ALL, None, None, None), P(), P(ALL, None), P(ALL))

    return jax.shard_map(local, mesh=grid, in_specs=in_specs, out_specs=P(ALL, None), check_vma=False)
```

```python
import functools
import math

import jax
import jax.numpy as jnp
from jax import lax
from jax.experimental import pallas as pl
from jax.experimental.pallas import tpu as pltpu
from jax.sharding import Mesh
from jax.sharding import PartitionSpec as P


HEAD = 128
REQ_TILES = 32
EXP_SCALE = math.log2(math.e) / math.sqrt(HEAD)
ALL = ("z", "y", "x", "c")
PLANE = ("y", "x", "c")
CAP = 2
CHUNKS = ((0,), (1, 2), (3,))
PLAN = ((), ((0, 1), (2, 3), 0), (1, 2, 3))


def request_table(dest_index, live_mask, count_dest, capacity, payload):
    onehot = (
        (dest_index[:, None] == jnp.arange(count_dest, dtype=jnp.int32)[None, :])
        & live_mask[:, None]
    ).astype(jnp.int32)
    rank_within = jnp.sum(onehot * (jnp.cumsum(onehot, axis=0) - 1), axis=1)
    target = jnp.where(live_mask, dest_index * capacity + rank_within, -1)
    slot_ids = jnp.arange(count_dest * capacity, dtype=jnp.int32)
    requests = jnp.max(
        jnp.where(target[:, None] == slot_ids[None, :], payload[:, None], 0), axis=0
    )
    return (requests.reshape(count_dest, capacity), dest_index * capacity + rank_within)


def score(queries, keys):
    return lax.dot_general(
        queries, keys, (((1,), (1,)), ((), ())), preferred_element_type=jnp.float32
    )


def weigh(scores, values_one, old_max, old_acc, masks):
    pieces = [scores[:, i : i + HEAD] for i in range(0, scores.shape[1], HEAD)]
    pieces = [
        piece if mask is None else jnp.where(mask, piece, -jnp.inf)
        for piece, mask in zip(pieces, masks, strict=True)
    ]
    top = jnp.max(functools.reduce(jnp.maximum, pieces), axis=1, keepdims=True)
    top = jnp.broadcast_to(top, pieces[0].shape)
    new_max = top if old_max is None else jnp.maximum(old_max, top)
    weights = [
        jnp.exp2((piece - new_max) * EXP_SCALE).astype(jnp.bfloat16) for piece in pieces
    ]
    acc = jnp.dot(
        jnp.concatenate(weights, axis=1), values_one, preferred_element_type=jnp.float32
    )
    if old_max is None:
        return new_max, acc[:, :HEAD], acc[:, HEAD:]
    fade = jnp.exp2((old_max - new_max) * EXP_SCALE)
    total, row_sum = old_acc
    return new_max, acc[:, :HEAD] + total * fade, acc[:, HEAD:] + row_sum * fade


def stack_heads(q_tile, repeat):
    return jnp.concatenate([q_tile[:, r * HEAD : (r + 1) * HEAD] for r in range(repeat)], axis=0)


def span_kernel(repeat, tile_rows, place_ref, q_ref, own_ref, *rest):
    earlier, (state_ref, key_buf, value_buf) = rest[:-3], rest[-3:]
    tiles = q_ref.shape[0] // tile_rows
    ones = jnp.ones((own_ref.shape[1], HEAD), jnp.bfloat16)
    other_ref, same_refs, first_ref = earlier[0], earlier[1:-1], earlier[-1]
    spans = [own_ref]
    for i, same_ref in enumerate(same_refs):
        spans += [other_ref.at[i], same_ref]
    for slot, ref in enumerate((*spans, first_ref)):
        key_buf[slot] = ref[0]
        value_buf[slot, :, :HEAD] = ref[1]
        value_buf[slot, :, HEAD:] = ones
    wide = repeat * tile_rows

    def own_scores(t):
        queries = stack_heads(q_ref[t * tile_rows : (t + 1) * tile_rows, :], repeat)
        return score(queries, key_buf[0, : (t + 1) * tile_rows])

    def put(t, state):
        for i, part in enumerate((*state[1:], state[0])):
            state_ref[0, t, :, i * HEAD : (i + 1) * HEAD] = part

    row = lax.rem(lax.broadcasted_iota(jnp.int32, (wide, tile_rows), 0), tile_rows)
    diagonal = lax.broadcasted_iota(jnp.int32, (wide, tile_rows), 1) <= row
    ahead = own_scores(0)
    for t in range(tiles):
        scores = ahead
        if t + 1 < tiles:
            ahead = own_scores(t + 1)
        masks = [None] * t + [diagonal]
        put(t, weigh(scores, value_buf[0, : (t + 1) * tile_rows], None, None, masks))

    def take(slot, carry):
        keys, values_one = key_buf[slot], value_buf[slot]

        def slot_scores(t):
            queries = stack_heads(q_ref[t * tile_rows : (t + 1) * tile_rows, :], repeat)
            return score(queries, keys)

        ahead = slot_scores(0)
        for t in range(tiles):
            scores = ahead
            if t + 1 < tiles:
                ahead = slot_scores(t + 1)
            old = [state_ref[0, t, :, i * HEAD : (i + 1) * HEAD] for i in range(3)]
            put(t, weigh(scores, values_one, old[2], old[:2], [None] * tiles))
        return carry

    lax.fori_loop(1, place_ref[0] + 1, take, 0)


def span_attention(heads, place, queries, own, earlier, tile_num):
    rows, width = queries.shape
    kv_heads = own.shape[2] // HEAD
    group = width // kv_heads
    repeat = group // HEAD
    tile_rows = rows // tile_num
    wide = repeat * tile_rows
    kv_spec = pl.BlockSpec((2, rows, HEAD), lambda g, place: (0, 0, heads[0] + g))
    other_spec = pl.BlockSpec(
        (earlier[0].shape[0], 2, rows, HEAD), lambda g, place: (0, 0, 0, heads[0] + g)
    )
    slots = len(earlier) + earlier[0].shape[0]
    return pl.pallas_call(
        functools.partial(span_kernel, repeat, tile_rows),
        out_shape=jax.ShapeDtypeStruct((len(heads), tile_num, wide, 3 * HEAD), jnp.float32),
        grid_spec=pltpu.PrefetchScalarGridSpec(
            num_scalar_prefetch=1,
            grid=(len(heads),),
            in_specs=[pl.BlockSpec((rows, group), lambda g, place: (0, heads[0] + g))]
            + [kv_spec, other_spec] + [kv_spec] * (len(earlier) - 1),
            out_specs=pl.BlockSpec((1, tile_num, wide, 3 * HEAD), lambda g, place: (g, 0, 0, 0)),
            scratch_shapes=[
                pltpu.VMEM((slots, rows, HEAD), jnp.bfloat16),
                pltpu.VMEM((slots, rows, 2 * HEAD), jnp.bfloat16),
            ],
        ),
        compiler_params=pltpu.CompilerParams(vmem_limit_bytes=56 * 2**20),
        cost_estimate=pl.CostEstimate(
            flops=4 * len(heads) * rows * group * rows * slots,
            bytes_accessed=len(heads) * (rows * group * 14 + slots * rows * 4 * HEAD),
            transcendentals=len(heads) * rows * repeat * rows * slots,
        ),
    )(place, queries, own, *earlier)


def listed_kernel(repeat, tile_rows, count_ref, pos_ref, q_ref, state_ref, block_ref, *rest):
    out_ref = rest[-1]
    tiles = q_ref.shape[0] // tile_rows
    list_len = pos_ref.shape[1]
    block_len = block_ref.shape[2]
    ones = jnp.ones((list_len * block_len, HEAD), jnp.bfloat16)

    def listed(t, kind):
        return jnp.concatenate([block_ref[pos_ref[t, i], kind] for i in range(list_len)], axis=0)

    def tile_rows_at(t):
        return pl.ds(pl.multiple_of(t * tile_rows, tile_rows), tile_rows)

    def tile_scores(t):
        return score(stack_heads(q_ref[tile_rows_at(t), :], repeat), listed(t, 0))

    def finish(t, scores):
        masks = [i < count_ref[t] for i in range(list_len)]
        old = [state_ref[0, t, :, i * HEAD : (i + 1) * HEAD] for i in range(3)]
        values_one = jnp.concatenate([listed(t, 1), ones], axis=1)
        _, total, row_sum = weigh(scores, values_one, old[2], old[:2], masks)
        result = (total / row_sum).astype(jnp.bfloat16)
        for r in range(repeat):
            out_ref[tile_rows_at(t), r * HEAD : (r + 1) * HEAD] = result[
                r * tile_rows : (r + 1) * tile_rows, :
            ]

    def pair(i, carry):
        first = tile_scores(2 * i)
        second = tile_scores(2 * i + 1)
        finish(2 * i, first)
        finish(2 * i + 1, second)
        return carry

    lax.fori_loop(0, tiles // 2, pair, 0)


def listed_attention(head, state_row, counts, position, queries, state, blocks, lane, partial_out):
    rows, width = queries.shape
    _, tile_num, wide, _ = state.shape
    group = wide * tile_num // rows * HEAD
    repeat = group // HEAD
    tile_rows = rows // tile_num
    in_specs = [
        pl.BlockSpec((rows, group), lambda t, c, p: (0, head)),
        pl.BlockSpec((1, tile_num, wide, 3 * HEAD), lambda t, c, p: (state_row, 0, 0, 0)),
        pl.BlockSpec((*blocks.shape[:3], HEAD), lambda t, c, p: (0, 0, 0, lane)),
    ]
    operands = [counts, position, queries, state, blocks]
    aliases = {}
    if partial_out is not None:
        in_specs.append(pl.BlockSpec(memory_space=pl.ANY))
        operands.append(partial_out)
        aliases = {5: 0}
    keys = position.shape[1] * blocks.shape[2]
    return pl.pallas_call(
        functools.partial(listed_kernel, repeat, tile_rows),
        out_shape=jax.ShapeDtypeStruct((rows, width), jnp.bfloat16),
        grid_spec=pltpu.PrefetchScalarGridSpec(
            num_scalar_prefetch=2,
            grid=(1,),
            in_specs=in_specs,
            out_specs=pl.BlockSpec((rows, group), lambda t, c, p: (0, head)),
        ),
        input_output_aliases=aliases,
        compiler_params=pltpu.CompilerParams(vmem_limit_bytes=40 * 2**20),
        cost_estimate=pl.CostEstimate(
            flops=4 * rows * group * keys,
            bytes_accessed=rows * group * 16 + blocks.size * 2,
            transcendentals=rows * repeat * keys,
        ),
    )(*operands)


def local(summary_q, summary_kv, kv_cache, block_slot, tile_blocks, tile_count):
    plane, groups, devices = (lax.axis_size(axes) for axes in (PLANE, "z", ALL))
    tile_num, list_len = tile_blocks.shape
    blk_dev = kv_cache.shape[0]
    req_devs = REQ_TILES // tile_num
    flat_index = lax.axis_index(ALL)
    entries = tile_blocks.reshape(-1)
    live_mask = (jnp.arange(list_len, dtype=jnp.int32)[None, :] < tile_count[:, None]).reshape(-1)
    block_ids = jnp.arange(block_slot.shape[0], dtype=jnp.int32)
    stored_at = jnp.sum(
        jnp.where(entries[:, None] == block_ids[None, :], block_slot[None, :], 0), axis=1
    )
    owner_dev = stored_at // blk_dev
    requests, position = request_table(
        owner_dev % plane,
        live_mask,
        plane,
        CAP,
        owner_dev // plane * blk_dev + stored_at % blk_dev,
    )
    asked = lax.all_to_all(requests, PLANE, split_axis=0, concat_axis=0, tiled=True)
    depth = (lax.axis_index("z") - asked // blk_dev + groups) % groups
    asked = depth * blk_dev + asked % blk_dev
    position = jnp.where(live_mask, position, 0).reshape(tile_num, list_len)
    place = (flat_index - 1 + req_devs) % req_devs
    own, asked = lax.optimization_barrier((summary_kv.transpose(1, 0, 2), asked))
    asked = asked.reshape(-1)

    def ahead(value, distance, takes):
        pairs = [
            (source, (source + distance) % devices)
            for source in range(devices)
            if takes((source - 1) % req_devs)
        ]
        return lax.ppermute(value, ALL, pairs)

    core = lax.axis_index("c")
    second = ahead(own, 2, lambda p: p + 2 <= req_devs)
    sixth = ahead(own, 6, lambda p: p + 6 <= req_devs)
    first = ahead(own, req_devs - 1, lambda p: p == 0)
    fourth = ahead(second, 2, lambda p: 2 <= p <= req_devs - 2)
    same = [second, fourth, sixth]
    give = [jnp.where(core == 0, a, b) for a, b in zip([own, *same[:-1]], same, strict=True)]
    other = lax.ppermute(jnp.stack(give), "c", [(0, 1), (1, 0)])
    earlier = [other, *same, first]

    def stack_column(heads):
        part = kv_cache[..., heads[0] * HEAD : (heads[-1] + 1) * HEAD]
        pieces = [part]
        for step in range(1, groups):
            pairs = [(source, (source + step) % groups) for source in range(groups)]
            pieces.append(lax.ppermute(part, "z", pairs))
        return jnp.concatenate(pieces, axis=0)

    columns = [stack_column(heads) for heads in CHUNKS]
    states, received, out = [], {}, None
    for turn, heads in enumerate(CHUNKS):
        column = columns[turn]
        if turn > 0:
            column, states, out = lax.optimization_barrier((column, states, out))
        arrived = lax.all_to_all(column[asked], PLANE, split_axis=0, concat_axis=0, tiled=True)
        for i, head in enumerate(heads):
            received[head] = (arrived, i)
        for task in PLAN[turn]:
            if isinstance(task, tuple):
                state = span_attention(task, place[None], summary_q, own, earlier, tile_num)
                states = states + [state]
            else:
                out = listed_attention(
                    task,
                    task % 2,
                    tile_count,
                    position,
                    summary_q,
                    states[task // 2],
                    *received[task],
                    out,
                )
    return out


def solution(mesh):
    grid = Mesh(mesh.devices.reshape(4, 4, 4, 2), ALL)
    in_specs = (P(ALL, None), P(ALL, None, None), P(ALL, None, None, None), P(), P(ALL, None), P(ALL))

    return jax.shard_map(local, mesh=grid, in_specs=in_specs, out_specs=P(ALL, None), check_vma=False)
```

```python
import functools
import math

import jax
import jax.numpy as jnp
from jax import lax
from jax.experimental import pallas as pl
from jax.experimental.pallas import tpu as pltpu
from jax.sharding import Mesh
from jax.sharding import PartitionSpec as P


HEAD = 128
REQ_TILES = 32
EXP_SCALE = math.log2(math.e) / math.sqrt(HEAD)
ALL = ("z", "y", "x", "c")
PLANE = ("y", "x", "c")
CAP = 2
CHUNKS = ((0,), (1, 2), (3,))
PLAN = ((), ((0, 1), (2, 3), 0), (1, 2, 3))


def request_table(dest_index, live_mask, count_dest, capacity, payload):
    onehot = (
        (dest_index[:, None] == jnp.arange(count_dest, dtype=jnp.int32)[None, :])
        & live_mask[:, None]
    ).astype(jnp.int32)
    rank_within = jnp.sum(onehot * (jnp.cumsum(onehot, axis=0) - 1), axis=1)
    target = jnp.where(live_mask, dest_index * capacity + rank_within, -1)
    slot_ids = jnp.arange(count_dest * capacity, dtype=jnp.int32)
    requests = jnp.max(
        jnp.where(target[:, None] == slot_ids[None, :], payload[:, None], 0), axis=0
    )
    return (requests.reshape(count_dest, capacity), dest_index * capacity + rank_within)


def score(queries, keys):
    return lax.dot_general(
        queries, keys, (((1,), (1,)), ((), ())), preferred_element_type=jnp.float32
    )


def weigh(scores, values_one, old_max, old_acc, masks):
    pieces = [scores[:, i : i + HEAD] for i in range(0, scores.shape[1], HEAD)]
    pieces = [
        piece if mask is None else jnp.where(mask, piece, -jnp.inf)
        for piece, mask in zip(pieces, masks, strict=True)
    ]
    top = jnp.max(functools.reduce(jnp.maximum, pieces), axis=1, keepdims=True)
    top = jnp.broadcast_to(top, pieces[0].shape)
    new_max = top if old_max is None else jnp.maximum(old_max, top)
    weights = [
        jnp.exp2((piece - new_max) * EXP_SCALE).astype(jnp.bfloat16) for piece in pieces
    ]
    acc = jnp.dot(
        jnp.concatenate(weights, axis=1), values_one, preferred_element_type=jnp.float32
    )
    if old_max is None:
        return new_max, acc[:, :HEAD], acc[:, HEAD:]
    fade = jnp.exp2((old_max - new_max) * EXP_SCALE)
    total, row_sum = old_acc
    return new_max, acc[:, :HEAD] + total * fade, acc[:, HEAD:] + row_sum * fade


def stack_heads(q_tile, repeat):
    return jnp.concatenate([q_tile[:, r * HEAD : (r + 1) * HEAD] for r in range(repeat)], axis=0)


def span_kernel(repeat, tile_rows, place_ref, q_ref, own_ref, *rest):
    earlier, (state_ref, key_buf, value_buf) = rest[:-3], rest[-3:]
    tiles = q_ref.shape[0] // tile_rows
    ones = jnp.ones((own_ref.shape[1], HEAD), jnp.bfloat16)
    other_ref, same_refs, first_ref = earlier[0], earlier[1:-1], earlier[-1]
    spans = [own_ref]
    for i, same_ref in enumerate(same_refs):
        spans += [other_ref.at[i], same_ref]
    for slot, ref in enumerate((*spans, first_ref)):
        key_buf[slot] = ref[0]
        value_buf[slot, :, :HEAD] = ref[1]
        value_buf[slot, :, HEAD:] = ones
    wide = repeat * tile_rows

    def own_scores(t):
        queries = stack_heads(q_ref[t * tile_rows : (t + 1) * tile_rows, :], repeat)
        return score(queries, key_buf[0, : (t + 1) * tile_rows])

    def put(t, state):
        for i, part in enumerate((*state[1:], state[0])):
            state_ref[0, t, :, i * HEAD : (i + 1) * HEAD] = part

    row = lax.rem(lax.broadcasted_iota(jnp.int32, (wide, tile_rows), 0), tile_rows)
    diagonal = lax.broadcasted_iota(jnp.int32, (wide, tile_rows), 1) <= row
    ahead = own_scores(0)
    for t in range(tiles):
        scores = ahead
        if t + 1 < tiles:
            ahead = own_scores(t + 1)
        masks = [None] * t + [diagonal]
        put(t, weigh(scores, value_buf[0, : (t + 1) * tile_rows], None, None, masks))

    def take(slot, carry):
        keys, values_one = key_buf[slot], value_buf[slot]

        def slot_scores(t):
            queries = stack_heads(q_ref[t * tile_rows : (t + 1) * tile_rows, :], repeat)
            return score(queries, keys)

        ahead = slot_scores(0)
        for t in range(tiles):
            scores = ahead
            if t + 1 < tiles:
                ahead = slot_scores(t + 1)
            old = [state_ref[0, t, :, i * HEAD : (i + 1) * HEAD] for i in range(3)]
            put(t, weigh(scores, values_one, old[2], old[:2], [None] * tiles))
        return carry

    lax.fori_loop(1, place_ref[0] + 1, take, 0)


def span_attention(heads, place, queries, own, earlier, tile_num):
    rows, width = queries.shape
    kv_heads = own.shape[2] // HEAD
    group = width // kv_heads
    repeat = group // HEAD
    tile_rows = rows // tile_num
    wide = repeat * tile_rows
    kv_spec = pl.BlockSpec((2, rows, HEAD), lambda g, place: (0, 0, heads[0] + g))
    other_spec = pl.BlockSpec(
        (earlier[0].shape[0], 2, rows, HEAD), lambda g, place: (0, 0, 0, heads[0] + g)
    )
    slots = len(earlier) + earlier[0].shape[0]
    return pl.pallas_call(
        functools.partial(span_kernel, repeat, tile_rows),
        out_shape=jax.ShapeDtypeStruct((len(heads), tile_num, wide, 3 * HEAD), jnp.float32),
        grid_spec=pltpu.PrefetchScalarGridSpec(
            num_scalar_prefetch=1,
            grid=(len(heads),),
            in_specs=[pl.BlockSpec((rows, group), lambda g, place: (0, heads[0] + g))]
            + [kv_spec, other_spec] + [kv_spec] * (len(earlier) - 1),
            out_specs=pl.BlockSpec((1, tile_num, wide, 3 * HEAD), lambda g, place: (g, 0, 0, 0)),
            scratch_shapes=[
                pltpu.VMEM((slots, rows, HEAD), jnp.bfloat16),
                pltpu.VMEM((slots, rows, 2 * HEAD), jnp.bfloat16),
            ],
        ),
        compiler_params=pltpu.CompilerParams(vmem_limit_bytes=56 * 2**20),
        cost_estimate=pl.CostEstimate(
            flops=4 * len(heads) * rows * group * rows * slots,
            bytes_accessed=len(heads) * (rows * group * 14 + slots * rows * 4 * HEAD),
            transcendentals=len(heads) * rows * repeat * rows * slots,
        ),
    )(place, queries, own, *earlier)


def listed_kernel(repeat, tile_rows, count_ref, pos_ref, q_ref, state_ref, block_ref, *rest):
    out_ref = rest[-1]
    tiles = q_ref.shape[0] // tile_rows
    list_len = pos_ref.shape[1]
    block_len = block_ref.shape[2]
    ones = jnp.ones((list_len * block_len, HEAD), jnp.bfloat16)

    def listed(t, kind):
        return jnp.concatenate([block_ref[pos_ref[t, i], kind] for i in range(list_len)], axis=0)

    def tile_rows_at(t):
        return pl.ds(pl.multiple_of(t * tile_rows, tile_rows), tile_rows)

    def tile_scores(t):
        return score(stack_heads(q_ref[tile_rows_at(t), :], repeat), listed(t, 0))

    def finish(t, scores):
        masks = [i < count_ref[t] for i in range(list_len)]
        old = [state_ref[0, t, :, i * HEAD : (i + 1) * HEAD] for i in range(3)]
        values_one = jnp.concatenate([listed(t, 1), ones], axis=1)
        _, total, row_sum = weigh(scores, values_one, old[2], old[:2], masks)
        result = (total / row_sum).astype(jnp.bfloat16)
        for r in range(repeat):
            out_ref[tile_rows_at(t), r * HEAD : (r + 1) * HEAD] = result[
                r * tile_rows : (r + 1) * tile_rows, :
            ]

    def pair(i, carry):
        first = tile_scores(2 * i)
        second = tile_scores(2 * i + 1)
        finish(2 * i, first)
        finish(2 * i + 1, second)
        return carry

    lax.fori_loop(0, tiles // 2, pair, 0)


def listed_attention(head, state_row, counts, position, queries, state, blocks, lane, partial_out):
    rows, width = queries.shape
    _, tile_num, wide, _ = state.shape
    group = wide * tile_num // rows * HEAD
    repeat = group // HEAD
    tile_rows = rows // tile_num
    in_specs = [
        pl.BlockSpec((rows, group), lambda t, c, p: (0, head)),
        pl.BlockSpec((1, tile_num, wide, 3 * HEAD), lambda t, c, p: (state_row, 0, 0, 0)),
        pl.BlockSpec((*blocks.shape[:3], HEAD), lambda t, c, p: (0, 0, 0, lane)),
    ]
    operands = [counts, position, queries, state, blocks]
    aliases = {}
    if partial_out is not None:
        in_specs.append(pl.BlockSpec(memory_space=pl.ANY))
        operands.append(partial_out)
        aliases = {5: 0}
    keys = position.shape[1] * blocks.shape[2]
    return pl.pallas_call(
        functools.partial(listed_kernel, repeat, tile_rows),
        out_shape=jax.ShapeDtypeStruct((rows, width), jnp.bfloat16),
        grid_spec=pltpu.PrefetchScalarGridSpec(
            num_scalar_prefetch=2,
            grid=(1,),
            in_specs=in_specs,
            out_specs=pl.BlockSpec((rows, group), lambda t, c, p: (0, head)),
        ),
        input_output_aliases=aliases,
        compiler_params=pltpu.CompilerParams(vmem_limit_bytes=40 * 2**20),
        cost_estimate=pl.CostEstimate(
            flops=4 * rows * group * keys,
            bytes_accessed=rows * group * 16 + blocks.size * 2,
            transcendentals=rows * repeat * keys,
        ),
    )(*operands)


def local(summary_q, summary_kv, kv_cache, block_slot, tile_blocks, tile_count):
    plane, groups, devices = (lax.axis_size(axes) for axes in (PLANE, "z", ALL))
    tile_num, list_len = tile_blocks.shape
    blk_dev = kv_cache.shape[0]
    req_devs = REQ_TILES // tile_num
    flat_index = lax.axis_index(ALL)
    entries = tile_blocks.reshape(-1)
    live_mask = (jnp.arange(list_len, dtype=jnp.int32)[None, :] < tile_count[:, None]).reshape(-1)
    block_ids = jnp.arange(block_slot.shape[0], dtype=jnp.int32)
    stored_at = jnp.sum(
        jnp.where(entries[:, None] == block_ids[None, :], block_slot[None, :], 0), axis=1
    )
    owner_dev = stored_at // blk_dev
    requests, position = request_table(
        owner_dev % plane,
        live_mask,
        plane,
        CAP,
        owner_dev // plane * blk_dev + stored_at % blk_dev,
    )
    asked = lax.all_to_all(requests, PLANE, split_axis=0, concat_axis=0, tiled=True)
    depth = (lax.axis_index("z") - asked // blk_dev + groups) % groups
    asked = depth * blk_dev + asked % blk_dev
    position = jnp.where(live_mask, position, 0).reshape(tile_num, list_len)
    place = (flat_index - 1 + req_devs) % req_devs
    own, asked = lax.optimization_barrier((summary_kv.transpose(1, 0, 2), asked))
    asked = asked.reshape(-1)

    def ahead(value, distance, takes):
        pairs = [
            (source, (source + distance) % devices)
            for source in range(devices)
            if takes((source - 1) % req_devs)
        ]
        return lax.ppermute(value, ALL, pairs)

    core = lax.axis_index("c")
    near = ahead(own, 2, lambda p: p + 2 < req_devs - 1)
    lifted = ahead(own, req_devs, lambda p: req_devs - 3 <= p <= req_devs - 2)
    fallen = ahead(lifted, 2 - req_devs, lambda p: req_devs - 3 <= p <= req_devs - 2)
    second = near + fallen
    sixth = ahead(own, 6, lambda p: p + 6 <= req_devs)
    first = ahead(own, req_devs - 1, lambda p: p == 0)
    fourth = ahead(near, 2, lambda p: 2 <= p <= req_devs - 2)
    same = [second, fourth, sixth]
    give = [jnp.where(core == 0, a, b) for a, b in zip([own, *same[:-1]], same, strict=True)]
    other = lax.ppermute(jnp.stack(give), "c", [(0, 1), (1, 0)])
    earlier = [other, *same, first]

    def stack_column(heads):
        part = kv_cache[..., heads[0] * HEAD : (heads[-1] + 1) * HEAD]
        pieces = [part]
        for step in range(1, groups):
            pairs = [(source, (source + step) % groups) for source in range(groups)]
            pieces.append(lax.ppermute(part, "z", pairs))
        return pieces

    columns = [stack_column(heads) for heads in CHUNKS]
    states, received, out = [], {}, None
    for turn, heads in enumerate(CHUNKS):
        column = columns[turn]
        if turn > 0:
            column, states, out = lax.optimization_barrier((column, states, out))
        column = jnp.concatenate(column, axis=0)
        arrived = lax.all_to_all(column[asked], PLANE, split_axis=0, concat_axis=0, tiled=True)
        for i, head in enumerate(heads):
            received[head] = (arrived, i)
        for task in PLAN[turn]:
            if isinstance(task, tuple):
                state = span_attention(task, place[None], summary_q, own, earlier, tile_num)
                states = states + [state]
            else:
                out = listed_attention(
                    task,
                    task % 2,
                    tile_count,
                    position,
                    summary_q,
                    states[task // 2],
                    *received[task],
                    out,
                )
    return out


def solution(mesh):
    grid = Mesh(mesh.devices.reshape(4, 4, 4, 2), ALL)
    in_specs = (P(ALL, None), P(ALL, None, None), P(ALL, None, None, None), P(), P(ALL, None), P(ALL))

    return jax.shard_map(local, mesh=grid, in_specs=in_specs, out_specs=P(ALL, None), check_vma=False)
```
